32 devices in a mesh: area: 8 (over y, x, core), layer: 4 (over z).
Axes of the slice: x: 2, y: 2, z: 4, core: 2. Of those that a mesh axis runs over, the one named last changes fastest.
Arguments:
- permeability: float32 [16, 4096, 512], P('layer', 'area'), may hold values from 0.1 to 10
- mobility: float32 [16, 4096, 512], P('layer', 'area'), may hold values from 0.3 to 3
- thickness: float32 [16], P('layer'), may hold values from 0.5 to 2
- caprock: int32 [4096, 512], P('area'), may hold values from 0 to 7
- plume: int32 [4096, 512], P('area'), may hold values from 0 to 15
- storage: float32 [4096, 512], P('area'), may hold values from 1.6 to 16
- source: float32 [4096, 512], P('area'), may hold values from -192 to 192
- pressure_old: float32 [4096, 512], P('area'), may hold values from -6 to 6
Outputs:
- cell_pressure: float32 [16, 4096, 512], P('layer', 'area')
- flux_rows: float32 [16, 4096, 512], P('layer', 'area')
- flux_cols: float32 [16, 4096, 512], P('layer', 'area')
The draws below stay inside these ranges and needn't reach their ends.
Inputs may be any that keep to these rules, and one draw needn't show every extreme that they name: Layers above layer caprock of a column are sealed rock. CO2 fills the open layers above layer plume of a column; where plume <= caprock a column holds no CO2.
All inputs are finite; a program needn't handle non-finite values.
Results may differ from the reference program's by a relative error of at most 0.0003.
Values sent between devices are 32-bit elements; how exact they have to be, the bound alone decides.
No kernel may reach another device: no remote copies, remote signals or barrier semaphores. Data moves between devices by JAX's collectives and lax.ppermute only.
A program may use at most 128 MiB of HBM per device.

```python
import math
import jax
import jax.numpy as jnp

NY = 512
SWEEPS = 3
NX = 4096
NZ = 16


def draw_source(key, part):
    rough_key = jax.random.fold_in(jax.random.fold_in(key, 11), 0)
    source_field = jax.random.truncated_normal(rough_key, -6.0, 6.0, (NX, NY), jnp.float32)
    return 2.0 * NZ * source_field


def with_ends(drawn, stream_key, low, largest):
    longest = drawn.shape.index(max(drawn.shape))
    spots = []
    for shift in (0, 1):
        where = [jax.random.randint(jax.random.fold_in(stream_key, axis), (), 0, length) for axis, length in enumerate(drawn.shape)]
        where[longest] = (where[longest] + shift) % drawn.shape[longest]
        spots.append(tuple(where))
    return drawn.at[spots[0]].set(low).at[spots[1]].set(largest)


def steps_of(own_key, shape, shards, low, high):
    factor_of = 1.0
    for dim, parts in shards:
        steps = jax.random.uniform(jax.random.fold_in(jax.random.fold_in(own_key, 6), dim), (parts,), jnp.float32, low / len(shards), high / len(shards))
        factor_of = factor_of * jnp.repeat(jnp.exp(steps), shape[dim] // parts).reshape((-1,) + (1,) * (len(shape) - 1 - dim))
    return factor_of


def normal_values(rng, extent, spread, reach, shards=(), kind=jnp.bfloat16):
    array = spread * jax.random.normal(rng, extent, jnp.float32)
    if shards:
        array = array * steps_of(rng, extent, shards, -0.22, 0.18)
    return jnp.clip(array, -reach, reach).astype(kind)


def setup_inputs(seed: int = 0) -> dict:
    key_list = jax.random.split(jax.random.key(seed), 9)
    permeability = jnp.clip(jnp.exp(math.log(10.0) - 4.6051702 * jax.random.uniform(key_list[0], (NZ, NX, NY), jnp.float32) ** steps_of(key_list[0], (NZ, NX, NY), ((0, 4), (1, 8)), -0.2, 0.2)), 0.1, 10.0)
    mobility = jnp.clip(jnp.exp(math.log(3.0) - 2.3025851 * jax.random.uniform(key_list[1], (NZ, NX, NY), jnp.float32) ** steps_of(key_list[1], (NZ, NX, NY), ((0, 4), (1, 8)), -0.2, 0.2)), 0.3, 3.0)
    thickness = jnp.clip(jnp.exp(math.log(2.0) - 1.3862944 * jax.random.uniform(key_list[2], (NZ,), jnp.float32) ** steps_of(key_list[2], (NZ,), ((0, 4),), -0.2, 0.2)), 0.5, 2.0)
    caprock = with_ends(jax.random.randint(key_list[3], (NX, NY), 0, NZ // 2), jax.random.fold_in(key_list[3], 1), 0, (NZ // 2) - 1).astype(jnp.int32)
    plume = with_ends(jax.random.randint(key_list[4], (NX, NY), 0, NZ), jax.random.fold_in(key_list[4], 1), 0, NZ - 1).astype(jnp.int32)
    storage = jnp.clip(jnp.exp(math.log(16.0) - 2.3025851 * jax.random.uniform(key_list[5], (NX, NY), jnp.float32) ** steps_of(key_list[5], (NX, NY), ((0, 8),), -0.2, 0.2)), 1.6, 16.0)
    source = draw_source(jax.random.fold_in(key_list[8], 71), 0)
    pressure_old = normal_values(key_list[7], (NX, NY), 1.0, 6.0, ((0, 8),), jnp.float32)
    return {"permeability": permeability, "mobility": mobility, "thickness": thickness, "caprock": caprock, "plume": plume, "storage": storage, "source": source, "pressure_old": pressure_old}


buoyancy_scale = 0.3
gravity_scale = 0.05
gas_density = 0.7
brine_density = 1.0


def harmonic(near_value, far_value):
    summed = near_value + far_value
    divisor = jnp.where(summed > 0, summed, 1.0)
    return 2.0 * near_value * far_value / divisor


def neighbours(padded, row_count):
    widened = jnp.pad(padded, ((0, 0), (1, 1)))
    return [widened[0:row_count, 1:-1], widened[2:row_count + 2, 1:-1],
            widened[1:row_count + 1, 0:-2], widened[1:row_count + 1, 2:]]


def prepare(summed_pad, storage, source, pressure_old):
    row_count = storage.shape[0]
    trans_pad = summed_pad[0]
    buoy_pad = summed_pad[1]
    drive_pad = buoyancy_scale * summed_pad[2]
    trans_faces = [harmonic(trans_pad[1:row_count + 1], neighbour) for neighbour in neighbours(trans_pad, row_count)]
    buoy_faces = [harmonic(buoy_pad[1:row_count + 1], neighbour) for neighbour in neighbours(buoy_pad, row_count)]
    drive_centre = drive_pad[1:row_count + 1]
    gravity_drive = sum(face_coef * (neighbour - drive_centre) for face_coef, neighbour in zip(buoy_faces, neighbours(drive_pad, row_count)))
    right_hand = storage * pressure_old + source + gravity_drive
    diagonal = storage + trans_faces[0] + trans_faces[1] + trans_faces[2] + trans_faces[3]
    return trans_faces, right_hand, diagonal


def relax(trans_faces, right_hand, diagonal, padded):
    row_count = right_hand.shape[0]
    inflow = sum(face_coef * neighbour for face_coef, neighbour in zip(trans_faces, neighbours(padded, row_count)))
    return (right_hand + inflow) / diagonal


def reference(permeability, mobility, thickness, caprock, plume, storage, source, pressure_old):
    layers = jnp.arange(NZ, dtype=jnp.int32)[:, None, None]
    open_cell = layers >= caprock[None]
    gas_cell = open_cell & (layers < plume[None])
    layer_thick = thickness[:, None, None]
    conduct = jnp.where(open_cell, permeability * mobility * layer_thick, 0.0)
    trans_col = jnp.sum(conduct, axis=0)
    buoy_col = jnp.sum(jnp.where(gas_cell, conduct, 0.0), axis=0)
    gas_height = jnp.sum(jnp.where(gas_cell, layer_thick, 0.0), axis=0)
    summed_pad = jnp.pad(jnp.stack([trans_col, buoy_col, gas_height]), ((0, 0), (1, 1), (0, 0)))
    trans_faces, right_hand, diagonal = prepare(summed_pad, storage, source, pressure_old)
    pressure = pressure_old
    for sweep_index in range(SWEEPS):
        pressure = relax(trans_faces, right_hand, diagonal, jnp.pad(pressure, ((1, 1), (0, 0))))
    layer_mass = layer_thick * jnp.where(gas_cell, gas_density, brine_density)
    hydro_head = jnp.cumsum(layer_mass, axis=0) - 0.5 * layer_mass
    cell_pressure = pressure[None] + gravity_scale * hydro_head
    next_conduct = jnp.pad(conduct[:, 1:, :], ((0, 0), (0, 1), (0, 0)))
    next_pressure = jnp.pad(cell_pressure[:, 1:, :], ((0, 0), (0, 1), (0, 0)))
    flux_rows = harmonic(conduct, next_conduct) * (cell_pressure - next_pressure)
    side_conduct = jnp.pad(conduct[:, :, 1:], ((0, 0), (0, 0), (0, 1)))
    side_pressure = jnp.pad(cell_pressure[:, :, 1:], ((0, 0), (0, 0), (0, 1)))
    flux_cols = harmonic(conduct, side_conduct) * (cell_pressure - side_pressure)
    return cell_pressure, flux_rows, flux_cols
```

```python
import functools

import jax
import jax.numpy as jnp
from jax import lax
from jax.experimental import pallas as pl
from jax.experimental.pallas import tpu as pltpu
from jax.sharding import PartitionSpec as P

SWEEPS = 3
CHUNKS = 4
PAD = 8

buoyancy_scale = 0.3
gravity_scale = 0.05
gas_density = 0.7
brine_density = 1.0

VM = pltpu.VMEM
SM = pltpu.SMEM
f32 = jnp.float32


def params(mib, grid_rank=0):
    kw = {}
    if grid_rank:
        kw["dimension_semantics"] = ("arbitrary",) * grid_rank
    return pltpu.CompilerParams(vmem_limit_bytes=mib << 20, **kw)


def harmonic(near_value, far_value):
    summed = near_value + far_value
    divisor = jnp.where(summed > 0, summed, 1.0)
    return 2.0 * near_value * far_value / divisor


def left_of(x):
    return pltpu.roll(x, x.shape[-1] - 1, 1)


def right_of(x):
    return pltpu.roll(x, 1, 1)


def last_lane(shape):
    return lax.broadcasted_iota(jnp.int32, shape, len(shape) - 1) == shape[-1] - 1


def conduct_of(perm, mob, thick, depth, cap):
    return jnp.where(depth >= cap, perm * mob * thick, 0.0)


def sums_rows(perm_ref, mob_ref, thick_ref, cap_ref, plume_ref, first, rows):
    cap, plume = cap_ref[rows, :], plume_ref[rows, :]
    trans = buoy = None
    for z in range(perm_ref.shape[0]):
        depth = first + z
        c = conduct_of(perm_ref[z, rows, :], mob_ref[z, rows, :], thick_ref[z], depth, cap)
        g = jnp.where(depth < plume, c, 0.0)
        trans = c if trans is None else trans + c
        buoy = g if buoy is None else buoy + g
    return trans, buoy


def sums_kernel(form, perm_ref, mob_ref, thick_ref, cap_ref, plume_ref, *rest):
    rows = perm_ref.shape[1]
    first = lax.axis_index("layer") * perm_ref.shape[0]
    halo_ref, out_ref = rest if form == "last" else (None, rest[0])

    def fill(offset):
        for r in range(0, rows, PAD):
            trans, buoy = sums_rows(
                perm_ref, mob_ref, thick_ref, cap_ref, plume_ref, first, slice(r, r + PAD)
            )
            if form == "first":
                out_ref[0, r : r + PAD, :] = trans
                out_ref[1, r : r + PAD, :] = buoy
            else:
                out_ref[0, 0, offset + r : offset + r + PAD, :] = trans
                out_ref[0, 1, offset + r : offset + r + PAD, :] = buoy

    if form != "last":
        fill(0)
        return

    @pl.when(pl.program_id(0) == 0)
    def _():
        out_ref[0, :, 0:PAD, :] = halo_ref[0]
        fill(PAD)

    @pl.when(pl.program_id(0) == 1)
    def _():
        fill(0)
        out_ref[0, :, rows : rows + PAD, :] = halo_ref[0]


def chunk_sums(form, index, chunks, perm, mob, thick, cap, plume, halo=None):
    layers, height, width = perm.shape
    rows = height // (2 * chunks)
    block = lambda s: chunks - 1 - index + s * (2 * index + 1)
    spec3 = pl.BlockSpec((layers, rows, width), lambda s: (0, block(s), 0))
    spec2 = pl.BlockSpec((rows, width), lambda s: (block(s), 0))
    in_specs = [spec3, spec3, pl.BlockSpec(memory_space=SM), spec2, spec2]
    args = [perm, mob, thick, cap, plume]
    out_rows = rows
    if form == "last":
        in_specs.append(pl.BlockSpec((1, 2, PAD, width), lambda s: (s, 0, 0, 0)))
        args.append(halo)
        out_rows = rows + PAD
    if form == "first":
        shape = (2, 2 * rows, width)
        out_spec = pl.BlockSpec((2, rows, width), lambda s: (0, s, 0))
    else:
        shape = (2, 2, out_rows, width)
        out_spec = pl.BlockSpec((1, 2, out_rows, width), lambda s: (s, 0, 0, 0))
    return pl.pallas_call(
        functools.partial(sums_kernel, form),
        grid=(2,),
        in_specs=in_specs,
        out_specs=out_spec,
        out_shape=jax.ShapeDtypeStruct(shape, f32),
        compiler_params=params(12, 1),
        name=f"sums_{index}",
    )(*args)


def edge_kernel(perm_a, mob_a, perm_b, mob_b, thick_ref, *rest):
    fields_a, fields_b = rest[0:5], rest[5:10]
    out_a, out_b = rest[10], rest[11]
    layers = perm_a.shape[0]
    first = lax.axis_index("layer") * layers
    rows = slice(0, PAD)
    for perm, mob, fields, out in (
        (perm_a, mob_a, fields_a, out_a),
        (perm_b, mob_b, fields_b, out_b),
    ):
        trans, buoy = sums_rows(perm, mob, thick_ref, fields[0], fields[1], first, rows)
        out[0] = trans
        out[1] = buoy
        for i, field in enumerate(fields):
            out[2 + i] = field[...].astype(f32)
    out_a[7] = jnp.zeros_like(out_a[7])
    for z in range(layers):
        out_a[7, z : z + 1, :] = conduct_of(
            perm_a[z, 0:1, :], mob_a[z, 0:1, :], thick_ref[z], first + z, fields_a[0][0:1, :]
        )


def edges(perm, mob, thick, fields):
    layers, height, width = perm.shape
    final = height // PAD - 1
    spec3 = lambda i: pl.BlockSpec((layers, PAD, width), lambda g: (0, i, 0))
    spec2 = lambda i: pl.BlockSpec((PAD, width), lambda g: (i, 0))
    whole = lambda n: pl.BlockSpec((n, PAD, width), lambda g: (0, 0, 0))
    return pl.pallas_call(
        edge_kernel,
        grid=(1,),
        in_specs=[spec3(0), spec3(0), spec3(final), spec3(final), pl.BlockSpec(memory_space=SM)]
        + [spec2(0)] * 5
        + [spec2(final)] * 5,
        out_specs=(whole(8), whole(7)),
        out_shape=(
            jax.ShapeDtypeStruct((8, PAD, width), f32),
            jax.ShapeDtypeStruct((7, PAD, width), f32),
        ),
        compiler_params=params(8, 1),
        name="edges",
    )(perm, mob, perm, mob, thick, *fields, *fields)


def thick_at(thick_ref, z, layers, count):
    shift = lax.rem(z // layers - lax.axis_index("layer") + count, count)
    return thick_ref[shift * layers + z % layers]


def window(index, chunks, rows, last):
    half = rows * chunks
    inner, outer = rows * index, rows * (index + 1) + (PAD if last else 0)
    reach = PAD if index == 0 else 2 * PAD
    return half - outer, half + inner - reach, outer - inner + reach


def prep_kernel(chunks, rows, layers, thick_ref, cap_ref, plume_ref, sto_ref, src_ref, old_ref, low_ref, high_ref, *outs):
    count = lax.axis_size("layer")
    upper = lax.axis_index("layer") >= count // 2
    thick = [thick_at(thick_ref, z, layers, count) for z in range(thick_ref.shape[0])]

    def fill(out, at, cap, plume, sto, src, old):
        height = jnp.zeros(cap.shape, f32)
        for z, t in enumerate(thick):
            height = height + jnp.where((cap <= z) & (plume > z), t, 0.0)
        n = cap.shape[0]
        out[0, pl.ds(at, n), :] = buoyancy_scale * height
        out[1, pl.ds(at, n), :] = jnp.where(sto > 0, sto, 1.0)
        out[2, pl.ds(at, n), :] = sto * old + src
        out[3, pl.ds(at, n), :] = old

    for index, out in enumerate(outs):
        last = index == chunks - 1
        a, b, length = window(index, chunks, rows, last)
        if last:
            a, length = a + PAD, length - PAD
        start = jnp.where(upper, b, a)
        base = jnp.where(upper, 0, PAD) if last else 0

        def step(g, _, start=start, base=base, out=out):
            at = pl.ds(pl.multiple_of(start + g * PAD, PAD), PAD)
            to = base + g * PAD
            if not isinstance(to, int):
                to = pl.multiple_of(to, PAD)
            fill(out, to, cap_ref[at, :], plume_ref[at, :], sto_ref[at, :], src_ref[at, :], old_ref[at, :])
            return 0

        lax.fori_loop(0, length // PAD, step, 0)
        if last:
            for flag, halo, to in ((~upper, low_ref, 0), (upper, high_ref, length)):

                @pl.when(flag)
                def _(halo=halo, to=to, out=out):
                    cap = halo[2].astype(jnp.int32)
                    plume = halo[3].astype(jnp.int32)
                    fill(out, to, cap, plume, halo[4], halo[5], halo[6])


def prepare(chunks, rows, layers, thick_all, fields, low, high):
    width = fields[0].shape[1]
    shapes = []
    for index in range(chunks):
        length = window(index, chunks, rows, index == chunks - 1)[2]
        shapes.append(jax.ShapeDtypeStruct((4, length, width), f32))
    return pl.pallas_call(
        functools.partial(prep_kernel, chunks, rows, layers),
        in_specs=[pl.BlockSpec(memory_space=SM)] + [pl.BlockSpec(memory_space=VM)] * 7,
        out_specs=tuple([pl.BlockSpec(memory_space=VM)] * chunks),
        out_shape=tuple(shapes),
        compiler_params=params(20),
        name="prepare",
    )(thick_all, *fields, low, high)


def solve_kernel(first, last, *refs):
    if first:
        own_ref, cross_ref, prep_ref, p_ref, carry_ref = refs[:5]
    else:
        own_ref, cross_ref, carry_in, prep_ref, p_ref, carry_ref = refs[:6]
    tb, fr, fc, qr, qc, rhs, inv, pa, pb = refs[-9:]
    count = lax.axis_size("layer")
    upper = lax.axis_index("layer") >= count // 2
    length, width = prep_ref.shape[1:]
    n = own_ref.shape[1]
    if first:
        for r in range(0, n, PAD):
            tb[:, PAD + r : 2 * PAD + r, :] = own_ref[:, r : r + PAD, :] + cross_ref[:, r : r + PAD, :]
    else:
        at = jnp.where(upper, 2 * PAD, 0) + PAD
        for r in range(0, n, PAD):
            tb[:, pl.ds(pl.multiple_of(at + r, PAD), PAD), :] = (
                own_ref[:, r : r + PAD, :] + cross_ref[:, r : r + PAD, :]
            )
        at = pl.multiple_of(jnp.where(upper, 0, n) + PAD, PAD)
        tb[:, pl.ds(at, 2 * PAD), :] = carry_in[...]
    tb[:, PAD + length : 2 * PAD + length, :] = jnp.zeros((2, PAD, width), f32)
    if not last:
        at = pl.multiple_of(jnp.where(upper, length - 2 * PAD, 0) + PAD, PAD)
        carry_ref[...] = tb[:, pl.ds(at, 2 * PAD), :]
    else:
        carry_ref[...] = jnp.zeros_like(carry_ref)

    edge = last_lane((PAD, width))
    zero = jnp.zeros((PAD, width), f32)
    fr[0:PAD, :] = zero
    qr[0:PAD, :] = zero
    for ref in (pa, pb):
        ref[0:PAD, :] = zero
        ref[PAD + length : 2 * PAD + length, :] = zero
    for r in range(0, length, PAD):
        here, down = slice(PAD + r, 2 * PAD + r), slice(PAD + r + 1, 2 * PAD + r + 1)
        t, b, d = tb[0, here, :], tb[1, here, :], prep_ref[0, r : r + PAD, :]
        fr[here, :] = harmonic(t, tb[0, down, :])
        fc[r : r + PAD, :] = jnp.where(edge, 0.0, harmonic(t, left_of(t)))
        if r + PAD < length:
            below = prep_ref[0, r + 1 : r + PAD + 1, :]
        else:
            below = pltpu.roll(d, PAD - 1, 0)
        qr[here, :] = harmonic(b, tb[1, down, :]) * (below - d)
        qc[r : r + PAD, :] = jnp.where(edge, 0.0, harmonic(b, left_of(b)) * (left_of(d) - d))
        pa[here, :] = prep_ref[3, r : r + PAD, :]
    for r in range(0, length, PAD):
        here, up = slice(PAD + r, 2 * PAD + r), slice(PAD + r - 1, 2 * PAD + r - 1)
        flow = qc[r : r + PAD, :]
        face = fc[r : r + PAD, :]
        rhs[r : r + PAD, :] = (
            prep_ref[2, r : r + PAD, :] + (qr[here, :] - qr[up, :]) + (flow - right_of(flow))
        )
        diagonal = prep_ref[1, r : r + PAD, :] + fr[up, :] + fr[here, :] + right_of(face) + face
        inv[r : r + PAD, :] = 1.0 / diagonal
    source, target = pa, pb
    for sweep in range(SWEEPS):
        final = sweep == SWEEPS - 1
        lo, hi = (PAD, PAD + p_ref.shape[0]) if final else (0, length)
        for r in range(lo, hi, PAD):
            here = slice(PAD + r, 2 * PAD + r)
            up = slice(PAD + r - 1, 2 * PAD + r - 1)
            down = slice(PAD + r + 1, 2 * PAD + r + 1)
            p, face = source[here, :], fc[r : r + PAD, :]
            value = (
                rhs[r : r + PAD, :]
                + fr[up, :] * source[up, :]
                + fr[here, :] * source[down, :]
                + right_of(face * p)
                + face * left_of(p)
            ) * inv[r : r + PAD, :]
            if final:
                p_ref[r - PAD : r, :] = value
            else:
                target[here, :] = value
        source, target = target, source


def solve(first, last, own, cross, carry, prep):
    length, width = prep.shape[1:]
    p_rows = length - PAD if last else length - 2 * PAD
    args = [own, cross] + ([] if first else [carry]) + [prep]
    tall = pltpu.VMEM((length + 2 * PAD, width), f32)
    flat = pltpu.VMEM((length, width), f32)
    return pl.pallas_call(
        functools.partial(solve_kernel, first, last),
        in_specs=[pl.BlockSpec(memory_space=VM)] * len(args),
        out_specs=(pl.BlockSpec(memory_space=VM), pl.BlockSpec(memory_space=VM)),
        out_shape=(
            jax.ShapeDtypeStruct((p_rows, width), f32),
            jax.ShapeDtypeStruct((2, 2 * PAD, width), f32),
        ),
        scratch_shapes=[pltpu.VMEM((2, length + 2 * PAD, width), f32), tall, flat, tall, flat, flat, flat, tall, tall],
        compiler_params=params(12),
        name="solve",
    )(*args)


def cells_kernel(perm_ref, mob_ref, cap_ref, plume_ref, perm_n, mob_n, cap_n, thick_ref, all_ref, high_ref, hr_ref, hc_ref, g_ref, gh_ref, cond):
    step, steps = pl.program_id(0), pl.num_programs(0)
    layers, rows, width = perm_ref.shape
    index, count = lax.axis_index("layer"), lax.axis_size("layer")
    first = index * layers
    top = [
        jnp.where(z < first, thick_at(all_ref, z, layers, count), 0.0)
        for z in range(all_ref.shape[0])
    ]

    def heads(cap, plume):
        over = jnp.zeros(cap.shape, f32)
        for z, t in enumerate(top):
            over = over + jnp.where((cap <= z) & (plume > z), gas_density * t, brine_density * t)
        out = []
        for z in range(layers):
            t = thick_ref[z]
            gas = (cap <= first + z) & (plume > first + z)
            mass = jnp.where(gas, t * gas_density, t * brine_density)
            out.append(gravity_scale * (over + 0.5 * mass))
            over = over + mass
        return out

    for r in range(0, rows, PAD):
        rr = slice(r, r + PAD)
        cap, plume = cap_ref[rr, :], plume_ref[rr, :]
        for z in range(layers):
            cond[z, rr, :] = conduct_of(perm_ref[z, rr, :], mob_ref[z, rr, :], thick_ref[z], first + z, cap)
        for z, h in enumerate(heads(cap, plume)):
            g_ref[z, rr, :] = h
    cap = cap_n[...]
    final = step == steps - 1
    for z in range(layers):
        inside = conduct_of(perm_n[z], mob_n[z], thick_ref[z], first + z, cap)
        cond[z, rows : rows + PAD, :] = inside

    @pl.when(final)
    def _():
        for z in range(layers):
            cond[z, rows : rows + 1, :] = high_ref[7, z : z + 1, :]
        for z, h in enumerate(heads(high_ref[2].astype(jnp.int32), high_ref[3].astype(jnp.int32))):
            gh_ref[z] = h

    edge = last_lane((PAD, width))
    for z in range(layers):
        for r in range(0, rows, PAD):
            c = cond[z, r : r + PAD, :]
            hr_ref[z, r : r + PAD, :] = harmonic(c, cond[z, r + 1 : r + PAD + 1, :])
            hc_ref[z, r : r + PAD, :] = jnp.where(edge, 0.0, harmonic(c, left_of(c)))


def cells(perm, mob, cap, plume, thick, thick_all, high, rows):
    layers, height, width = perm.shape
    steps = height // rows
    per = rows // PAD
    nxt = lambda i: jnp.minimum((i + 1) * per, height // PAD - 1)
    spec3 = pl.BlockSpec((layers, rows, width), lambda i: (0, i, 0))
    spec2 = pl.BlockSpec((rows, width), lambda i: (i, 0))
    next3 = pl.BlockSpec((layers, PAD, width), lambda i: (0, nxt(i), 0))
    next2 = pl.BlockSpec((PAD, width), lambda i: (nxt(i), 0))
    smem = pl.BlockSpec(memory_space=SM)
    full = jax.ShapeDtypeStruct(perm.shape, f32)
    return pl.pallas_call(
        cells_kernel,
        grid=(steps,),
        in_specs=[spec3, spec3, spec2, spec2, next3, next3, next2, smem, smem,
                  pl.BlockSpec((8, PAD, width), lambda i: (0, 0, 0))],
        out_specs=(spec3, spec3, spec3, pl.BlockSpec((layers, PAD, width), lambda i: (0, 0, 0))),
        out_shape=(full, full, full, jax.ShapeDtypeStruct((layers, PAD, width), f32)),
        scratch_shapes=[pltpu.VMEM((layers, rows + PAD, width), f32)],
        compiler_params=params(16, 1),
        name="cells",
    )(perm, mob, cap, plume, perm, mob, cap, thick, thick_all, high)


def output_kernel(chunks, unit, *refs):
    parts = refs[:chunks]
    hr_ref, hc_ref, g_ref, gn_ref, gh_ref, cp_ref, fr_ref, fc_ref, pfull, cp = refs[chunks:]
    step, steps = pl.program_id(0), pl.num_programs(0)
    layers, rows, width = hr_ref.shape
    half = unit * chunks

    @pl.when(step == 0)
    def _():
        count = lax.axis_size("layer")
        upper = (lax.axis_index("layer") >= count // 2).astype(jnp.int32)
        for index, part in enumerate(parts):
            last = index == chunks - 1
            a, b, length = window(index, chunks, unit, last)
            n = length - 2 * PAD
            pfull[a + PAD : a + PAD + n, :] = part[upper, 0:n, :]
            n = length - PAD if last else n
            pfull[b + PAD : b + PAD + n, :] = part[1 - upper, 0:n, :]

    start = pl.multiple_of(step * rows, PAD)
    for z in range(layers):
        for r in range(0, rows, PAD):
            value = pfull[pl.ds(start + r, PAD), :] + g_ref[z, r : r + PAD, :]
            cp[z, r : r + PAD, :] = value
            cp_ref[z, r : r + PAD, :] = value
        beyond = jnp.where(step == steps - 1, gh_ref[z], gn_ref[z])
        cp[z, rows : rows + PAD, :] = pfull[pl.ds(start + rows, PAD), :] + beyond
        for r in range(0, rows, PAD):
            here = cp[z, r : r + PAD, :]
            fr_ref[z, r : r + PAD, :] = hr_ref[z, r : r + PAD, :] * (here - cp[z, r + 1 : r + PAD + 1, :])
            fc_ref[z, r : r + PAD, :] = hc_ref[z, r : r + PAD, :] * (here - left_of(here))


def outputs(parts, hr, hc, g, gh, unit, rows):
    layers, height, width = hr.shape
    chunks = len(parts)
    steps = height // rows
    per = rows // PAD
    nxt = lambda i: jnp.minimum((i + 1) * per, height // PAD - 1)
    spec3 = pl.BlockSpec((layers, rows, width), lambda i: (0, i, 0))
    full = jax.ShapeDtypeStruct(hr.shape, f32)
    return pl.pallas_call(
        functools.partial(output_kernel, chunks, unit),
        grid=(steps,),
        in_specs=[pl.BlockSpec(memory_space=VM)] * chunks
        + [spec3, spec3, spec3, pl.BlockSpec((layers, PAD, width), lambda i: (0, nxt(i), 0)),
           pl.BlockSpec((layers, PAD, width), lambda i: (0, 0, 0))],
        out_specs=(spec3, spec3, spec3),
        out_shape=(full, full, full),
        scratch_shapes=[pltpu.VMEM((height + PAD, width), f32), pltpu.VMEM((layers, rows + PAD, width), f32)],
        compiler_params=params(20, 1),
        name="outputs",
    )(*parts, hr, hc, g, g, gh)


def local(permeability, mobility, thickness, caprock, plume, storage, source, pressure_old):
    layers, height, width = permeability.shape
    count = lax.axis_size("layer")
    tiles = lax.axis_size("area")
    half = count // 2
    chunks = CHUNKS
    unit = height // (2 * chunks)
    index = lax.axis_index("layer")
    upper = (index >= half).astype(jnp.int32)
    middle = (index == half - 1) | (index == half)
    fields = (caprock, plume, storage, source, pressure_old)

    forward = [(i, i + 1) for i in range(tiles - 1)]
    backward = [(i + 1, i) for i in range(tiles - 1)]
    inward = [[(h, h + 1), (count - 1 - h, count - 2 - h)] for h in range(half - 1)]
    outward = [[(b, a) for a, b in pairs] for pairs in inward[::-1]]
    swap = [(half - 1, half), (half, half - 1)]

    def send_in(own):
        total = own
        for pairs in inward:
            total = own + lax.ppermute(total, "layer", pairs)
        return total

    def cross_first(total):
        n = unit + PAD
        near = lax.dynamic_slice_in_dim(total, upper * (unit - PAD), n, 1)
        far = lax.dynamic_slice_in_dim(total, (1 - upper) * (unit - PAD), n, 1)
        return near, lax.ppermute(far, "layer", swap)

    def cross_next(total):
        near = lax.dynamic_index_in_dim(total, upper, 0, keepdims=False)
        far = lax.dynamic_index_in_dim(total, 1 - upper, 0, keepdims=False)
        return near, lax.ppermute(far, "layer", swap)

    own = [chunk_sums("first", 0, chunks, permeability, mobility, thickness, caprock, plume)]
    edge_first, edge_last = edges(permeability, mobility, thickness, fields)
    low = lax.ppermute(edge_last, "area", forward)
    high = lax.ppermute(edge_first, "area", backward)
    for j in range(1, chunks - 1):
        own.append(chunk_sums("mid", j, chunks, permeability, mobility, thickness, caprock, plume))
    halo = jnp.stack([low[0:2], high[0:2]])
    own.append(chunk_sums("last", chunks - 1, chunks, permeability, mobility, thickness, caprock, plume, halo))

    blocks = [thickness]
    for s in range(1, count):
        blocks.append(lax.ppermute(thickness, "layer", [(i, (i - s) % count) for i in range(count)]))
    thick_all = jnp.concatenate(blocks)

    preps = prepare(chunks, unit, layers, thick_all, fields, low, high)
    hr, hc, g, gh = cells(permeability, mobility, caprock, plume, thickness, thick_all, high, 64)

    parts = []
    carry = None
    for j in range(chunks):
        total = send_in(own[j])
        near, cross = cross_first(total) if j == 0 else cross_next(total)
        value, carry = solve(j == 0, j == chunks - 1, near, cross, carry, preps[j])
        other = lax.ppermute(value, "layer", swap)
        both = jnp.stack([value, other])
        if outward:
            sent, got = both, None
            for pairs in outward:
                sent = lax.ppermute(sent, "layer", pairs)
                got = sent if got is None else got + sent
            both = jnp.where(middle, both, got)
        parts.append(both)
    return outputs(parts, hr, hc, g, gh, unit, 64)


def solution(mesh):
    in_specs = (
        P("layer", "area", None),
        P("layer", "area", None),
        P("layer"),
        P("area", None),
        P("area", None),
        P("area", None),
        P("area", None),
        P("area", None),
    )
    out_specs = (P("layer", "area", None), P("layer", "area", None), P("layer", "area", None))
    return jax.shard_map(local, mesh=mesh, in_specs=in_specs, out_specs=out_specs, check_vma=False)
```

```python
import functools

import jax
import jax.numpy as jnp
from jax import lax
from jax.experimental import pallas as pl
from jax.experimental.pallas import tpu as pltpu
from jax.sharding import PartitionSpec as P

SWEEPS = 3
CHUNKS = 4
PAD = 8

buoyancy_scale = 0.3
gravity_scale = 0.05
gas_density = 0.7
brine_density = 1.0

VM = pltpu.VMEM
SM = pltpu.SMEM
f32 = jnp.float32
ANY = pl.BlockSpec(memory_space=pl.ANY)
WHOLE = pl.BlockSpec(memory_space=VM)
SCALARS = pl.BlockSpec(memory_space=SM)


def params(mib, grid_rank=0):
    kw = {}
    if grid_rank:
        kw["dimension_semantics"] = ("arbitrary",) * grid_rank
    return pltpu.CompilerParams(vmem_limit_bytes=mib << 20, **kw)


def call(kernel, args, specs, after, **kw):
    n, extra = len(args), len(after)

    def body(*refs):
        kernel(*refs[:n], *refs[n + extra :])

    return pl.pallas_call(body, in_specs=list(specs) + [ANY] * extra, **kw)(*args, *after)


def harmonic(near_value, far_value):
    return 2.0 * near_value * far_value / jnp.maximum(near_value + far_value, 1e-30)


def next_col(x):
    return pltpu.roll(x, x.shape[-1] - 1, 1)


def prev_col(x):
    return pltpu.roll(x, 1, 1)


def last_lane(shape):
    return lax.broadcasted_iota(jnp.int32, shape, len(shape) - 1) == shape[-1] - 1


def split(half):
    groups = half // PAD
    final = max(1, groups // 8)
    rest = groups - final
    sizes = [rest // (CHUNKS - 1) + (i < rest % (CHUNKS - 1)) for i in range(CHUNKS - 1)]
    return [PAD * g for g in sizes + [final]]


def upper_half():
    return lax.axis_index("layer") >= lax.axis_size("layer") // 2


class Plan:
    def __init__(self, height):
        self.height, self.half = height, height // 2
        self.sizes = split(self.half)
        self.count = len(self.sizes)
        self.inner = [sum(self.sizes[:j]) for j in range(self.count)]

    def strips(self, j):
        return self.half - self.inner[j] - self.sizes[j], self.half + self.inner[j]

    def window(self, j):
        inner = self.inner[j]
        outer = inner + self.sizes[j] + (PAD if j == self.count - 1 else 0)
        reach = PAD if j == 0 else 2 * PAD
        return self.half - outer, self.half + inner - reach, outer - inner + reach


def conduct_of(perm, mob, thick, depth, cap):
    return jnp.where(depth >= cap, perm * mob * thick, 0.0)


def sums_rows(perm_ref, mob_ref, thick_ref, cap_ref, plume_ref, first, rows):
    cap, plume = cap_ref[rows, :], plume_ref[rows, :]
    trans = buoy = None
    for z in range(perm_ref.shape[0]):
        depth = first + z
        c = conduct_of(perm_ref[z, rows, :], mob_ref[z, rows, :], thick_ref[z], depth, cap)
        g = jnp.where(depth < plume, c, 0.0)
        trans = c if trans is None else trans + c
        buoy = g if buoy is None else buoy + g
    return trans, buoy


def sums_kernel(form, perm_ref, mob_ref, thick_ref, cap_ref, plume_ref, *rest):
    layers, rows, width = perm_ref.shape
    first = lax.axis_index("layer") * layers
    out_ref = rest[-1]
    step = pl.program_id(0)

    def fill(put):
        for r in range(0, rows, PAD):
            put(r, *sums_rows(perm_ref, mob_ref, thick_ref, cap_ref, plume_ref, first, slice(r, r + PAD)))

    if form == "first":
        def put(r, trans, buoy):
            at = pl.ds(pl.multiple_of(PAD + step * rows + r, PAD), PAD)
            out_ref[0, at, :] = trans
            out_ref[1, at, :] = buoy

        fill(put)
        lane = lax.broadcasted_iota(jnp.int32, (PAD, width), 1)
        slab = jnp.zeros((PAD, width), f32)
        for z in range(layers):
            slab = jnp.where(lane == first + z, thick_ref[z], slab)
        at = pl.ds(pl.multiple_of(step * (2 * rows + PAD), PAD), PAD)
        out_ref[0, at, :] = slab
        out_ref[1, at, :] = slab
        return

    def put_at(offset):
        def put(r, trans, buoy):
            out_ref[0, 0, offset + r : offset + r + PAD, :] = trans
            out_ref[0, 1, offset + r : offset + r + PAD, :] = buoy
        return put

    if form == "mid":
        fill(put_at(0))
        return
    halo_ref = rest[0]

    @pl.when(step == 0)
    def _():
        out_ref[0, :, 0:PAD, :] = halo_ref[0]
        fill(put_at(PAD))

    @pl.when(step == 1)
    def _():
        fill(put_at(0))
        out_ref[0, :, rows : rows + PAD, :] = halo_ref[0]


def chunk_sums(plan, j, perm, mob, thick, cap, plume, halo, after):
    layers, height, width = perm.shape
    form = "first" if j == 0 else "last" if j == plan.count - 1 else "mid"
    rows = plan.sizes[j]
    low, high = plan.strips(j)
    start = lambda s: (low // PAD + s * ((high - low) // PAD)) * PAD
    E = pl.Element
    spec3 = pl.BlockSpec((E(layers), E(rows), E(width)), lambda s: (0, start(s), 0))
    spec2 = pl.BlockSpec((E(rows), E(width)), lambda s: (start(s), 0))
    specs = [spec3, spec3, SCALARS, spec2, spec2]
    args = [perm, mob, thick, cap, plume]
    out_rows = rows
    if form == "last":
        specs.append(pl.BlockSpec((1, 2, PAD, width), lambda s: (s, 0, 0, 0)))
        args.append(halo)
        out_rows = rows + PAD
    if form == "first":
        shape = (2, 2 * rows + 2 * PAD, width)
        out_spec = pl.BlockSpec(shape, lambda s: (0, 0, 0))
    else:
        shape = (2, 2, out_rows, width)
        out_spec = pl.BlockSpec((1, 2, out_rows, width), lambda s: (s, 0, 0, 0))
    return call(
        functools.partial(sums_kernel, form), args, specs, after,
        grid=(2,),
        out_specs=out_spec,
        out_shape=jax.ShapeDtypeStruct(shape, f32),
        compiler_params=params(12, 1),
        name=f"sums_{j}",
    )


def edge_kernel(perm_a, mob_a, perm_b, mob_b, thick_ref, *rest):
    fields_a, fields_b = rest[0:5], rest[5:10]
    out_a, out_b = rest[10], rest[11]
    layers = perm_a.shape[0]
    first = lax.axis_index("layer") * layers
    for perm, mob, fields, out in (
        (perm_a, mob_a, fields_a, out_a),
        (perm_b, mob_b, fields_b, out_b),
    ):
        trans, buoy = sums_rows(perm, mob, thick_ref, fields[0], fields[1], first, slice(0, PAD))
        out[0] = trans
        out[1] = buoy
        for i, field in enumerate(fields):
            out[2 + i] = field[...].astype(f32)
    slabs = -(-layers // PAD)
    for i in range(slabs):
        out_a[7 + i] = jnp.zeros_like(out_a[7 + i])
    for z in range(layers):
        row = conduct_of(
            perm_a[z, 0:1, :], mob_a[z, 0:1, :], thick_ref[z], first + z, fields_a[0][0:1, :]
        )
        out_a[7 + z // PAD, z % PAD : z % PAD + 1, :] = row


def edges(perm, mob, thick, fields, after):
    layers, height, width = perm.shape
    final = height // PAD - 1
    spec3 = lambda i: pl.BlockSpec((layers, PAD, width), lambda g: (0, i, 0))
    spec2 = lambda i: pl.BlockSpec((PAD, width), lambda g: (i, 0))
    whole = lambda n: pl.BlockSpec((n, PAD, width), lambda g: (0, 0, 0))
    tall = 7 + -(-layers // PAD)
    specs = [spec3(0), spec3(0), spec3(final), spec3(final), SCALARS]
    specs += [spec2(0)] * 5 + [spec2(final)] * 5
    return call(
        edge_kernel, (perm, mob, perm, mob, thick, *fields, *fields), specs, after,
        grid=(1,),
        out_specs=(whole(tall), whole(7)),
        out_shape=(
            jax.ShapeDtypeStruct((tall, PAD, width), f32),
            jax.ShapeDtypeStruct((7, PAD, width), f32),
        ),
        compiler_params=params(8, 1),
        name="edges",
    )


def prep_kernel(plan, thick_ref, cap_ref, plume_ref, sto_ref, src_ref, old_ref, low_ref, high_ref, *outs):
    upper = upper_half()
    thick = [thick_ref[z] for z in range(thick_ref.shape[0])]

    def fill(out, at, cap, plume, sto, src, old):
        height = jnp.zeros(cap.shape, f32)
        for z, t in enumerate(thick):
            height = height + jnp.where((cap <= z) & (plume > z), t, 0.0)
        out[0, pl.ds(at, PAD), :] = buoyancy_scale * height
        out[1, pl.ds(at, PAD), :] = jnp.where(sto > 0, sto, 1.0)
        out[2, pl.ds(at, PAD), :] = sto * old + src
        out[3, pl.ds(at, PAD), :] = old

    for j, out in enumerate(outs):
        last = j == plan.count - 1
        a, b, length = plan.window(j)
        if last:
            a, length = a + PAD, length - PAD
        start = jnp.where(upper, b, a)
        base = jnp.where(upper, 0, PAD) if last else 0

        def step(g, _, start=start, base=base, out=out):
            at = pl.ds(pl.multiple_of(start + g * PAD, PAD), PAD)
            to = pl.multiple_of(base + g * PAD, PAD)
            fill(out, to, cap_ref[at, :], plume_ref[at, :], sto_ref[at, :], src_ref[at, :], old_ref[at, :])
            return 0

        lax.fori_loop(0, length // PAD, step, 0)
        if last:
            for flag, halo, to in ((~upper, low_ref, 0), (upper, high_ref, length)):

                @pl.when(flag)
                def _(halo=halo, to=to, out=out):
                    cap = halo[2].astype(jnp.int32)
                    plume = halo[3].astype(jnp.int32)
                    fill(out, to, cap, plume, halo[4], halo[5], halo[6])


def prepare(plan, thick_all, fields, low, high, after):
    width = fields[0].shape[1]
    shapes = [jax.ShapeDtypeStruct((4, plan.window(j)[2], width), f32) for j in range(plan.count)]
    return call(
        functools.partial(prep_kernel, plan), (thick_all, *fields, low, high),
        [SCALARS] + [WHOLE] * 7, after,
        out_specs=tuple([WHOLE] * plan.count),
        out_shape=tuple(shapes),
        compiler_params=params(16),
        name="prepare",
    )


def solve_kernel(first, last, pieces, *refs):
    sums, refs = refs[:pieces], refs[pieces:]
    if not first:
        carry_in, refs = refs[0], refs[1:]
    prep_ref, p_ref, carry_ref = refs[:3]
    tb, fr, fc, qr, qc, rhs, inv, pa, pb = refs[3:]
    index, half = lax.axis_index("layer"), lax.axis_size("layer") // 2
    upper = index >= half
    middle = (index == half - 1) | (index == half)
    length, width = prep_ref.shape[1:]

    def total(at):
        value = sums[0][:, at, :]
        for ref in sums[1:]:
            value = value + ref[:, at, :]
        return value

    if first:
        at = jnp.where(upper, 0, PAD)
        for r in range(0, length, PAD):
            tb[:, PAD + r : 2 * PAD + r, :] = total(pl.ds(pl.multiple_of(at + r, PAD), PAD))
        at = pl.multiple_of(jnp.where(upper, length, 0), PAD)
        slab = total(pl.ds(at, PAD))[0]
        p_ref[length - 2 * PAD : length - PAD, :] = jnp.where(middle, slab, 0.0)
    else:
        n = length - 2 * PAD
        at = jnp.where(upper, 2 * PAD, 0) + PAD
        for r in range(0, n, PAD):
            tb[:, pl.ds(pl.multiple_of(at + r, PAD), PAD), :] = total(slice(r, r + PAD))
        at = pl.multiple_of(jnp.where(upper, 0, n) + PAD, PAD)
        tb[:, pl.ds(at, 2 * PAD), :] = carry_in[...]
    tb[:, PAD + length : 2 * PAD + length, :] = jnp.zeros((2, PAD, width), f32)
    if last:
        carry_ref[...] = jnp.zeros_like(carry_ref)
    else:
        at = pl.multiple_of(jnp.where(upper, length - 2 * PAD, 0) + PAD, PAD)
        carry_ref[...] = tb[:, pl.ds(at, 2 * PAD), :]

    edge = last_lane((PAD, width))
    zero = jnp.zeros((PAD, width), f32)
    fr[0:PAD, :] = zero
    qr[0:PAD, :] = zero
    for ref in (pa, pb):
        ref[0:PAD, :] = zero
        ref[PAD + length : 2 * PAD + length, :] = zero
    for r in range(0, length, PAD):
        here, down = slice(PAD + r, 2 * PAD + r), slice(PAD + r + 1, 2 * PAD + r + 1)
        t, b, d = tb[0, here, :], tb[1, here, :], prep_ref[0, r : r + PAD, :]
        fr[here, :] = harmonic(t, tb[0, down, :])
        fc[r : r + PAD, :] = jnp.where(edge, 0.0, harmonic(t, next_col(t)))
        if r + PAD < length:
            below = prep_ref[0, r + 1 : r + PAD + 1, :]
        else:
            below = pltpu.roll(d, PAD - 1, 0)
        qr[here, :] = harmonic(b, tb[1, down, :]) * (below - d)
        qc[r : r + PAD, :] = jnp.where(edge, 0.0, harmonic(b, next_col(b)) * (next_col(d) - d))
        pa[here, :] = prep_ref[3, r : r + PAD, :]
    for r in range(0, length, PAD):
        here, up = slice(PAD + r, 2 * PAD + r), slice(PAD + r - 1, 2 * PAD + r - 1)
        flow = qc[r : r + PAD, :]
        face = fc[r : r + PAD, :]
        rhs[r : r + PAD, :] = (
            prep_ref[2, r : r + PAD, :] + (qr[here, :] - qr[up, :]) + (flow - prev_col(flow))
        )
        diagonal = prep_ref[1, r : r + PAD, :] + fr[up, :] + fr[here, :] + prev_col(face) + face
        inv[r : r + PAD, :] = 1.0 / diagonal
    source, target = pa, pb
    for sweep in range(SWEEPS):
        final = sweep == SWEEPS - 1
        lo, hi = (PAD, length if last else length - PAD) if final else (0, length)
        for r in range(lo, hi, PAD):
            here = slice(PAD + r, 2 * PAD + r)
            up = slice(PAD + r - 1, 2 * PAD + r - 1)
            down = slice(PAD + r + 1, 2 * PAD + r + 1)
            p, face = source[here, :], fc[r : r + PAD, :]
            value = (
                rhs[r : r + PAD, :]
                + fr[up, :] * source[up, :]
                + fr[here, :] * source[down, :]
                + prev_col(face * p)
                + face * next_col(p)
            ) * inv[r : r + PAD, :]
            if final:
                p_ref[r - PAD : r, :] = jnp.where(middle, value, 0.0)
            else:
                target[here, :] = value
        source, target = target, source


def solve(first, last, sums, carry, prep, after):
    length, width = prep.shape[1:]
    p_rows = length - PAD if first or last else length - 2 * PAD
    args = list(sums) + ([] if first else [carry]) + [prep]
    tall = pltpu.VMEM((length + 2 * PAD, width), f32)
    flat = pltpu.VMEM((length, width), f32)
    return call(
        functools.partial(solve_kernel, first, last, len(sums)), args, [WHOLE] * len(args), after,
        out_specs=(WHOLE, WHOLE),
        out_shape=(
            jax.ShapeDtypeStruct((p_rows, width), f32),
            jax.ShapeDtypeStruct((2, 2 * PAD, width), f32),
        ),
        scratch_shapes=[pltpu.VMEM((2, length + 2 * PAD, width), f32), tall, flat, tall, flat, flat, flat, tall, tall],
        compiler_params=params(10),
        name="solve",
    )


def local_heads(first, thick_ref, cap, plume):
    over, out = None, []
    for z in range(thick_ref.shape[0]):
        t = thick_ref[z]
        gas = (cap <= first + z) & (plume > first + z)
        mass = jnp.where(gas, t * gas_density, t * brine_density)
        mid = 0.5 * mass
        out.append(gravity_scale * (mid if over is None else over + mid))
        over = mass if over is None else over + mass
    return out


def cells_kernel(final_piece, perm_ref, mob_ref, cap_ref, plume_ref, perm_n, mob_n, cap_n, thick_ref, high_ref, hr_ref, hc_ref, g_ref, gh_ref, cond):
    layers, rows, width = perm_ref.shape
    first = lax.axis_index("layer") * layers
    for r in range(0, rows, PAD):
        rr = slice(r, r + PAD)
        cap, plume = cap_ref[rr, :], plume_ref[rr, :]
        for z in range(layers):
            cond[z, rr, :] = conduct_of(perm_ref[z, rr, :], mob_ref[z, rr, :], thick_ref[z], first + z, cap)
        for z, h in enumerate(local_heads(first, thick_ref, cap, plume)):
            g_ref[z, rr, :] = h
    cap = cap_n[...]
    for z in range(layers):
        cond[z, rows : rows + PAD, :] = conduct_of(perm_n[z], mob_n[z], thick_ref[z], first + z, cap)
    if final_piece:
        @pl.when(pl.program_id(0) == pl.num_programs(0) - 1)
        def _():
            for z in range(layers):
                cond[z, rows : rows + 1, :] = high_ref[7 + z // PAD, z % PAD : z % PAD + 1, :]
            cap, plume = high_ref[2].astype(jnp.int32), high_ref[3].astype(jnp.int32)
            for z, h in enumerate(local_heads(first, thick_ref, cap, plume)):
                gh_ref[z] = h
    else:
        gh_ref[...] = jnp.zeros_like(gh_ref)

    edge = last_lane((PAD, width))
    for z in range(layers):
        for r in range(0, rows, PAD):
            c = cond[z, r : r + PAD, :]
            hr_ref[z, r : r + PAD, :] = harmonic(c, cond[z, r + 1 : r + PAD + 1, :])
            hc_ref[z, r : r + PAD, :] = jnp.where(edge, 0.0, harmonic(c, next_col(c)))


def cells(perm, mob, cap, plume, thick, high, base, steps, rows, after):
    layers, height, width = perm.shape
    per = rows // PAD
    nxt = lambda i: jnp.minimum((base + i + 1) * per, height // PAD - 1)
    spec3 = pl.BlockSpec((layers, rows, width), lambda i: (0, base + i, 0))
    spec2 = pl.BlockSpec((rows, width), lambda i: (base + i, 0))
    next3 = pl.BlockSpec((layers, PAD, width), lambda i: (0, nxt(i), 0))
    next2 = pl.BlockSpec((PAD, width), lambda i: (nxt(i), 0))
    out3 = pl.BlockSpec((layers, rows, width), lambda i: (0, i, 0))
    full = jax.ShapeDtypeStruct((layers, rows * steps, width), f32)
    final = (base + steps) * rows == height
    return call(
        functools.partial(cells_kernel, final), (perm, mob, cap, plume, perm, mob, cap, thick, high),
        [spec3, spec3, spec2, spec2, next3, next3, next2, SCALARS, pl.BlockSpec(high.shape, lambda i: (0, 0, 0))],
        after,
        grid=(steps,),
        out_specs=(out3, out3, out3, pl.BlockSpec((layers, PAD, width), lambda i: (0, 0, 0))),
        out_shape=(full, full, full, jax.ShapeDtypeStruct((layers, PAD, width), f32)),
        scratch_shapes=[pltpu.VMEM((layers, rows + PAD, width), f32)],
        compiler_params=params(14, 1),
        name="cells",
    )


def tops_kernel(layers, thick_ref, cap_ref, plume_ref, high_ref, out_ref):
    first = lax.axis_index("layer") * layers
    thick = [jnp.where(z < first, thick_ref[z], 0.0) for z in range(thick_ref.shape[0])]

    def value(cap, plume):
        over = jnp.zeros(cap.shape, f32)
        for z, t in enumerate(thick):
            over = over + jnp.where((cap <= z) & (plume > z), gas_density * t, brine_density * t)
        return gravity_scale * over

    height = cap_ref.shape[0]

    def step(g, _):
        at = pl.ds(pl.multiple_of(g * PAD, PAD), PAD)
        out_ref[at, :] = value(cap_ref[at, :], plume_ref[at, :])
        return 0

    lax.fori_loop(0, height // PAD, step, 0)
    out_ref[height : height + PAD, :] = value(high_ref[2].astype(jnp.int32), high_ref[3].astype(jnp.int32))


def tops(layers, thick_all, cap, plume, high, after):
    height, width = cap.shape
    return call(
        functools.partial(tops_kernel, layers), (thick_all, cap, plume, high),
        [SCALARS, WHOLE, WHOLE, WHOLE], after,
        out_specs=WHOLE,
        out_shape=jax.ShapeDtypeStruct((height + PAD, width), f32),
        compiler_params=params(6),
        name="tops",
    )


def output_kernel(plan, chunks, groups, pieces, spans, fresh, *refs):
    count = plan.count
    parts = []
    for _ in chunks:
        near, far = refs[: groups[0]], refs[groups[0] : sum(groups)]
        refs = refs[sum(groups) :]
        parts.append((near, far))
    cells_refs = [refs[3 * i : 3 * i + 3] for i in range(len(pieces))]
    refs = refs[3 * len(pieces) :]
    gh_ref, top_ref, refs = refs[0], refs[1], refs[2:]
    if not fresh:
        refs = refs[3:]
    outs, refs = refs[:3], refs[3:]
    pfull, cp, slots, sems = refs
    layers, block, width = slots.shape[2:]
    upper = upper_half()

    def summed(group, r):
        value = group[0][r : r + PAD, :]
        for ref in group[1:]:
            value = value + ref[r : r + PAD, :]
        return value

    for j, (near, far) in zip(chunks, parts):
        last = j == count - 1
        a, b, length = plan.window(j)
        n = length - (PAD if last else 2 * PAD)

        def place(low, high, a=a, b=b, n=n, last=last):
            for r in range(0, n, PAD):
                if not (last and r == n - PAD):
                    at = a + PAD + r
                    pfull[at : at + PAD, :] = summed(low, r) + top_ref[at : at + PAD, :]
                at = b + PAD + r
                pfull[at : at + PAD, :] = summed(high, r) + top_ref[at : at + PAD, :]

        @pl.when(upper)
        def _():
            place(far, near)

        @pl.when(~upper)
        def _():
            place(near, far)

    def piece_of(row):
        base = 0
        for i, size in enumerate(pieces):
            if row < base + size:
                return cells_refs[i], row - base
            base += size
        return None, None

    blocks = []
    for lo, hi in spans:
        while lo < hi:
            base = 0
            for size in pieces:
                if lo < base + size:
                    break
                base += size
            end = min(hi, base + size, lo + block)
            blocks.append((lo, end))
            lo = end

    copies = {}
    for k, (lo, hi) in enumerate(blocks):
        slot, rows = k % 2, hi - lo
        if k >= 2:
            for c in copies.pop(k - 2):
                c.wait()
        (hr, hc, g), off = piece_of(lo)
        (ng, noff) = piece_of(hi)
        for z in range(layers):
            for r in range(0, rows, PAD):
                value = pfull[lo + r : lo + r + PAD, :] + g[z, off + r : off + r + PAD, :]
                cp[z, r : r + PAD, :] = value
                slots[slot, 0, z, r : r + PAD, :] = value
            beyond = gh_ref[z] if ng is None else ng[2][z, noff : noff + PAD, :]
            cp[z, rows : rows + PAD, :] = pfull[hi : hi + PAD, :] + beyond
            for r in range(0, rows, PAD):
                here = cp[z, r : r + PAD, :]
                at = slice(off + r, off + r + PAD)
                slots[slot, 1, z, r : r + PAD, :] = hr[z, at, :] * (here - cp[z, r + 1 : r + PAD + 1, :])
                slots[slot, 2, z, r : r + PAD, :] = hc[z, at, :] * (here - next_col(here))
        copies[k] = [
            pltpu.make_async_copy(
                slots.at[slot, i, :, 0:rows, :], outs[i].at[:, lo:hi, :], sems.at[slot, i]
            )
            for i in range(3)
        ]
        for c in copies[k]:
            c.start()
    for k in sorted(copies):
        for c in copies[k]:
            c.wait()


def outputs(plan, chunks, parts, pieces, gh, top, spans, done, after):
    layers, _, width = pieces[0][0].shape
    groups = (len(parts[0][0]), len(parts[0][1]))
    args = [x for j in chunks for group in parts[j] for x in group]
    args += [x for piece in pieces for x in piece]
    args += [gh, top]
    specs = [WHOLE] * len(args)
    aliases = {}
    if done is not None:
        aliases = {len(args) + i: i for i in range(3)}
        args += list(done)
        specs += [ANY] * 3
    block = 64
    full = jax.ShapeDtypeStruct((layers, plan.height, width), f32)
    sizes = [piece[0].shape[1] for piece in pieces]
    return call(
        functools.partial(output_kernel, plan, chunks, groups, sizes, spans, done is None), args, specs, after,
        out_specs=(ANY, ANY, ANY),
        out_shape=(full, full, full),
        input_output_aliases=aliases,
        scratch_shapes=[
            pltpu.VMEM((plan.height + PAD, width), f32),
            pltpu.VMEM((layers, block + PAD, width), f32),
            pltpu.VMEM((2, 3, layers, block, width), f32),
            pltpu.SemaphoreType.DMA((2, 3)),
        ],
        compiler_params=params(24),
        name="outputs",
    )


def local(permeability, mobility, thickness, caprock, plume, storage, source, pressure_old):
    keep = lambda x: pltpu.with_memory_space_constraint(x, pltpu.HBM)
    permeability, mobility, cap, plm = [keep(x) for x in (permeability, mobility, caprock, plume)]
    layers, height, width = permeability.shape
    count = lax.axis_size("layer")
    tiles = lax.axis_size("area")
    half = count // 2
    depth = layers * count
    plan = Plan(height)
    index = lax.axis_index("layer")
    upper = (index >= half).astype(jnp.int32)
    fields = (caprock, plume, storage, source, pressure_old)

    forward = [(i, i + 1) for i in range(tiles - 1)]
    backward = [(i + 1, i) for i in range(tiles - 1)]
    mirror = lambda pairs: pairs + [(count - 1 - a, count - 1 - b) for a, b in pairs]
    inward = [mirror([(h, h + 1)]) for h in range(half - 1)]
    near_in = [mirror([(h, half - 1)]) for h in range(half - 1)]
    far_in = [mirror([(h, half)]) for h in range(half - 1)]
    swap = mirror([(half - 1, half)])
    out_near = [mirror([(half - 1, h)]) for h in range(half - 1)]
    out_far = [mirror([(half, h)]) for h in range(half - 1)]
    send = lambda x, pairs: lax.ppermute(x, "layer", pairs)

    def chain(own):
        terms = [own]
        for pairs in inward:
            total = terms[0] if len(terms) == 1 else terms[0] + terms[1]
            terms = [own, send(total, pairs)]
        return terms

    def strip(x, far):
        if x.ndim == 3:
            n = plan.sizes[0] + 2 * PAD
            at = (1 - upper if far else upper) * (x.shape[1] - n)
            return lax.dynamic_slice_in_dim(x, at, n, 1)
        return lax.dynamic_index_in_dim(x, 1 - upper if far else upper, 0, keepdims=False)

    def cross(terms):
        far = sum(strip(x, True) for x in terms)
        near = sum(strip(x, False) for x in terms)
        return far, [near, send(far, swap)]

    def spread(value):
        near = [value] + [send(value, pairs) for pairs in out_near]
        far = [send(value, swap)] + [send(value, pairs) for pairs in out_far]
        return near, far

    sums = lambda j, halo, after: chunk_sums(
        plan, j, permeability, mobility, thickness, cap, plm, halo, after
    )
    last = plan.count - 1
    own = [sums(0, None, [])]
    edge_first, edge_last = edges(permeability, mobility, thickness, [keep(x) for x in fields], [own[0]])
    low = lax.ppermute(edge_last, "area", forward)
    high = lax.ppermute(edge_first, "area", backward)
    for j in range(1, last):
        own.append(sums(j, None, [own[-1] if j > 1 else edge_first]))
    halo = jnp.stack([low[0:2], high[0:2]])
    own.append(sums(last, halo, [own[-1]]))
    terms = [chain(x) for x in own[:last]]
    near_last, far_last = strip(own[last], False), strip(own[last], True)
    final = [near_last]
    final += [send(near_last, pairs) for pairs in near_in]
    final += [send(far_last, pairs) for pairs in far_in]
    final += [send(far_last, swap)]

    block = 64
    steps = height // block
    cuts = [steps * 3 // 8, steps * 6 // 8, steps]
    cell = lambda i, after: cells(
        permeability, mobility, cap, plm, thickness, high,
        cuts[i - 1] if i else 0, cuts[i] - (cuts[i - 1] if i else 0), block, after,
    )

    far0, sums0 = cross(terms[0])
    piece0 = cell(0, [far0, near_last, far_last])
    far1, sums1 = cross(terms[1])
    row = upper * (plan.sizes[0] + PAD)
    thick_all = sum(lax.dynamic_slice(x, (0, row, 0), (1, 1, depth)) for x in sums0)[0, 0]
    preps = prepare(plan, thick_all, fields, low, high, [piece0[0], far1])
    parts = []
    value, carry = solve(True, False, sums0, None, preps[0], [])
    parts.append(spread(value))
    slab = plan.sizes[0] - PAD
    thick_top = sum(x[slab, 0:depth] for x in parts[0][0])
    piece1 = cell(1, [value])
    after = piece1[0]
    ready = (sums1,)
    for j in range(1, last):
        if j > 1:
            far, ready_j = cross(terms[j])
        else:
            far, ready_j = far1, sums1
        value, carry = solve(False, False, ready_j, carry, preps[j], [after])
        parts.append(spread(value))
        if j == 1:
            piece2 = cell(2, [value])
            top = tops(layers, thick_top, caprock, plume, high, [piece2[0]])
            after = top
        else:
            after = value
    value, carry = solve(False, True, final, carry, preps[last], [after])
    parts.append(spread(value))

    pieces = [piece0[:3], piece1[:3], piece2[:3]]
    gh = piece2[3]
    reach = plan.inner[last]
    lo, hi = plan.half - reach + PAD, plan.half + reach - 2 * PAD
    done = outputs(plan, list(range(last)), parts, pieces, gh, top, [(lo, hi)], None, [value])
    return outputs(plan, [last - 1, last], parts, pieces, gh, top, [(0, lo), (hi, height)], done, [])


def solution(mesh):
    in_specs = (
        P("layer", "area", None),
        P("layer", "area", None),
        P("layer"),
        P("area", None),
        P("area", None),
        P("area", None),
        P("area", None),
        P("area", None),
    )
    out_specs = (P("layer", "area", None), P("layer", "area", None), P("layer", "area", None))
    return jax.shard_map(local, mesh=mesh, in_specs=in_specs, out_specs=out_specs, check_vma=False)
```

```python
import functools

import jax
import jax.numpy as jnp
from jax import lax
from jax.experimental import pallas as pl
from jax.experimental.pallas import tpu as pltpu
from jax.sharding import PartitionSpec as P


SWEEPS = 3
MIDDLE, FINAL = 9, 15
PAD = 8

buoyancy_scale = 0.3
gravity_scale = 0.05
gas_density = 0.7
brine_density = 1.0

VM = pltpu.VMEM
SM = pltpu.SMEM
f32 = jnp.float32
ANY = pl.BlockSpec(memory_space=pl.ANY)
WHOLE = pl.BlockSpec(memory_space=VM)
SCALARS = pl.BlockSpec(memory_space=SM)


def params(mib, grid_rank=0):
    kw = {}
    if grid_rank:
        kw["dimension_semantics"] = ("arbitrary",) * grid_rank
    return pltpu.CompilerParams(vmem_limit_bytes=mib << 20, **kw)


def call(kernel, args, specs, after, **kw):
    n, extra = len(args), len(after)

    def body(*refs):
        kernel(*refs[:n], *refs[n + extra :])

    return pl.pallas_call(body, in_specs=list(specs) + [ANY] * extra, **kw)(*args, *after)


def harmonic(near_value, far_value):
    return 2.0 * near_value * far_value / jnp.maximum(near_value + far_value, 1e-30)


def next_col(x):
    return pltpu.roll(x, x.shape[-1] - 1, 1)


def prev_col(x):
    return pltpu.roll(x, 1, 1)


def last_lane(shape):
    return lax.broadcasted_iota(jnp.int32, shape, len(shape) - 1) == shape[-1] - 1


def split(half):
    groups = half // PAD
    final = max(1, groups * FINAL // 32)
    mid = max(1, groups * MIDDLE // 32)
    return [PAD * g for g in (groups - mid - final, mid, final)]


def scale():
    return max(1, lax.axis_size("layer") // 4)


def upper_half():
    return lax.axis_index("layer") >= lax.axis_size("layer") // 2


class Plan:
    def __init__(self, height):
        self.height, self.half = height, height // 2
        self.sizes = split(self.half)
        self.count = len(self.sizes)
        self.inner = [sum(self.sizes[:j]) for j in range(self.count)]

    def strips(self, j):
        return self.half - self.inner[j] - self.sizes[j], self.half + self.inner[j]

    def window(self, j):
        inner = self.inner[j]
        outer = inner + self.sizes[j] + (PAD if j == self.count - 1 else 0)
        reach = PAD if j == 0 else 2 * PAD
        return self.half - outer, self.half + inner - reach, outer - inner + reach


def conduct_of(perm, mob, thick, depth, cap):
    return jnp.where(depth >= cap, perm * mob * thick, 0.0)


def sums_rows(perm_ref, mob_ref, thick_ref, cap_ref, plume_ref, first, rows):
    cap, plume = cap_ref[rows, :], plume_ref[rows, :]
    trans = buoy = None
    for z in range(perm_ref.shape[0]):
        depth = first + z
        c = conduct_of(perm_ref[z, rows, :], mob_ref[z, rows, :], thick_ref[z], depth, cap)
        g = jnp.where(depth < plume, c, 0.0)
        trans = c if trans is None else trans + c
        buoy = g if buoy is None else buoy + g
    return trans, buoy


def sums_kernel(form, perm_ref, mob_ref, thick_ref, cap_ref, plume_ref, *rest):
    layers, rows, width = perm_ref.shape
    first = lax.axis_index("layer") * layers
    out_ref = rest[-1]
    step = pl.program_id(0)

    def fill(put):
        for r in range(0, rows, PAD):
            put(r, *sums_rows(perm_ref, mob_ref, thick_ref, cap_ref, plume_ref, first, slice(r, r + PAD)))

    if form == "first":
        def put(r, trans, buoy):
            at = pl.ds(pl.multiple_of(PAD + step * rows + r, PAD), PAD)
            out_ref[0, at, :] = trans
            out_ref[1, at, :] = buoy

        fill(put)
        lane = lax.broadcasted_iota(jnp.int32, (PAD, width), 1)
        slab = jnp.zeros((PAD, width), f32)
        for z in range(layers):
            slab = jnp.where(lane == first + z, thick_ref[z], slab)
        out_ref[0, 0:PAD, :] = slab
        out_ref[1, 0:PAD, :] = slab
        return

    def put_at(offset):
        def put(r, trans, buoy):
            out_ref[0, 0, offset + r : offset + r + PAD, :] = trans
            out_ref[0, 1, offset + r : offset + r + PAD, :] = buoy

        return put

    if form == "mid":
        fill(put_at(0))
        return
    halo_ref, near_ref, far_ref = rest
    upper = upper_half()

    def put_in(ref, offset):
        def put(r, trans, buoy):
            ref[0, offset + r : offset + r + PAD, :] = trans
            ref[1, offset + r : offset + r + PAD, :] = buoy

        return put

    for ref, near in ((near_ref, True), (far_ref, False)):
        for strip in range(2):
            mine = upper == (strip == 1) if near else upper == (strip == 0)

            @pl.when((step == strip) & mine)
            def _(ref=ref, strip=strip):
                fill(put_in(ref, PAD * (1 - strip)))
                ref[:, strip * rows : strip * rows + PAD, :] = halo_ref[0]


def chunk_sums(plan, j, perm, mob, thick, cap, plume, halo, after):
    layers, _, width = perm.shape
    form = "first" if j == 0 else "last" if j == plan.count - 1 else "mid"
    rows = plan.sizes[j]
    low, high = plan.strips(j)
    start = lambda s: (low // PAD + s * ((high - low) // PAD)) * PAD
    E = pl.Element
    spec3 = pl.BlockSpec((E(layers), E(rows), E(width)), lambda s: (0, start(s), 0))
    spec2 = pl.BlockSpec((E(rows), E(width)), lambda s: (start(s), 0))
    specs = [spec3, spec3, SCALARS, spec2, spec2]
    args = [perm, mob, thick, cap, plume]
    out_rows = rows
    if form == "last":
        specs.append(pl.BlockSpec((1, 2, PAD, width), lambda s: (s, 0, 0, 0)))
        args.append(halo)
        out_rows = rows + PAD
    if form == "first":
        shape = (2, 2 * rows + PAD, width)
        out_spec = pl.BlockSpec(shape, lambda s: (0, 0, 0))
    elif form == "last":
        shape = (2, out_rows, width)
        out_spec = pl.BlockSpec(shape, lambda s: (0, 0, 0))
    else:
        shape = (2, 2, out_rows, width)
        out_spec = pl.BlockSpec((1, 2, out_rows, width), lambda s: (s, 0, 0, 0))
    if form == "last":
        out_spec, shape = (out_spec, out_spec), [shape, shape]
    else:
        shape = [shape]
    kinds = tuple(jax.ShapeDtypeStruct(x, f32) for x in shape)
    return call(
        functools.partial(sums_kernel, form), args, specs, after,
        grid=(2,),
        out_specs=out_spec,
        out_shape=kinds if form == "last" else kinds[0],
        compiler_params=params(8, 1),
        name=f"sums_{j}",
    )


def edge_kernel(perm_a, mob_a, perm_b, mob_b, thick_ref, *rest):
    fields_a, fields_b = rest[0:5], rest[5:10]
    out_a, out_b = rest[10], rest[11]
    layers = perm_a.shape[0]
    first = lax.axis_index("layer") * layers
    for perm, mob, fields, out in (
        (perm_a, mob_a, fields_a, out_a),
        (perm_b, mob_b, fields_b, out_b),
    ):
        trans, buoy = sums_rows(perm, mob, thick_ref, fields[0], fields[1], first, slice(0, PAD))
        out[0] = trans
        out[1] = buoy
        for i, field in enumerate(fields):
            out[2 + i] = field[...].astype(f32)
    slabs = -(-layers // PAD)
    for i in range(slabs):
        out_a[7 + i] = jnp.zeros_like(out_a[7 + i])
    for z in range(layers):
        row = conduct_of(
            perm_a[z, 0:1, :], mob_a[z, 0:1, :], thick_ref[z], first + z, fields_a[0][0:1, :]
        )
        out_a[7 + z // PAD, z % PAD : z % PAD + 1, :] = row


def edges(perm, mob, thick, fields, after):
    layers, height, width = perm.shape
    final = height // PAD - 1
    spec3 = lambda i: pl.BlockSpec((layers, PAD, width), lambda g: (0, i, 0))
    spec2 = lambda i: pl.BlockSpec((PAD, width), lambda g: (i, 0))
    whole = lambda n: pl.BlockSpec((n, PAD, width), lambda g: (0, 0, 0))
    tall = 7 + -(-layers // PAD)
    specs = [spec3(0), spec3(0), spec3(final), spec3(final), SCALARS]
    specs += [spec2(0)] * 5 + [spec2(final)] * 5
    return call(
        edge_kernel, (perm, mob, perm, mob, thick, *fields, *fields), specs, after,
        grid=(1,),
        out_specs=(whole(tall), whole(7)),
        out_shape=(
            jax.ShapeDtypeStruct((tall, PAD, width), f32),
            jax.ShapeDtypeStruct((7, PAD, width), f32),
        ),
        compiler_params=params(4, 1),
        name="edges",
    )


def merge_kernel(pieces, *refs):
    terms, (near_ref, far_ref) = refs[:pieces], refs[pieces:]
    upper = upper_half().astype(jnp.int32)
    for out, side in ((far_ref, 1 - upper), (near_ref, upper)):
        rows = out.shape[1]
        for r in range(0, rows, PAD):
            value = None
            for ref in terms:
                if len(ref.shape) == 3:
                    at = side * (ref.shape[1] - rows) + r if r else 0
                    x = ref[:, pl.ds(pl.multiple_of(at, PAD) if r else 0, PAD), :]
                else:
                    x = ref[side, :, r : r + PAD, :]
                value = x if value is None else value + x
            out[:, r : r + PAD, :] = value


def merge(plan, terms, after):
    width = terms[0].shape[-1]
    rows = plan.sizes[0] + 2 * PAD if terms[0].ndim == 3 else terms[0].shape[2]
    kind = jax.ShapeDtypeStruct((2, rows, width), f32)
    return call(
        functools.partial(merge_kernel, len(terms)), terms, [WHOLE] * len(terms), after,
        out_specs=(WHOLE, WHOLE),
        out_shape=(kind, kind),
        compiler_params=params(4),
        name="merge",
    )


def prep_kernel(plan, cap_ref, plume_ref, sto_ref, src_ref, old_ref, low_ref, high_ref, *outs):
    upper = upper_half()

    def fill(out, at, cap, plume, sto, src, old):
        out[0, pl.ds(at, PAD), :] = cap.astype(f32)
        out[1, pl.ds(at, PAD), :] = jnp.where(sto > 0, sto, 1.0)
        out[2, pl.ds(at, PAD), :] = sto * old + src
        out[3, pl.ds(at, PAD), :] = old
        out[4, pl.ds(at, PAD), :] = plume.astype(f32)

    for j, out in enumerate(outs):
        last = j == plan.count - 1
        a, b, length = plan.window(j)
        if last:
            a, length = a + PAD, length - PAD
        start = jnp.where(upper, b, a)
        base = jnp.where(upper, 0, PAD) if last else 0

        def step(g, _, start=start, base=base, out=out):
            at = pl.ds(pl.multiple_of(start + g * PAD, PAD), PAD)
            to = pl.multiple_of(base + g * PAD, PAD)
            fill(out, to, cap_ref[at, :], plume_ref[at, :], sto_ref[at, :], src_ref[at, :], old_ref[at, :])
            return 0

        lax.fori_loop(0, length // PAD, step, 0)
        if last:
            for flag, halo, to in ((~upper, low_ref, 0), (upper, high_ref, length)):

                @pl.when(flag)
                def _(halo=halo, to=to, out=out):
                    fill(out, to, halo[2], halo[3], halo[4], halo[5], halo[6])


def prepare(plan, fields, low, high, after):
    width = fields[0].shape[1]
    shapes = [jax.ShapeDtypeStruct((5, plan.window(j)[2], width), f32) for j in range(plan.count)]
    return call(
        functools.partial(prep_kernel, plan), (*fields, low, high),
        [WHOLE] * 7, after,
        out_specs=tuple([WHOLE] * plan.count),
        out_shape=tuple(shapes),
        compiler_params=params(4),
        name="prepare",
    )


def solve_kernel(first, last, prefixed, pieces, *refs):
    thick_ref, sums, refs = refs[0], refs[1 : 1 + pieces], refs[1 + pieces :]
    if not first:
        carry_in, refs = refs[0], refs[1:]
    before = 0
    if prefixed:
        before_ref, refs = refs[0], refs[1:]
        before = before_ref.shape[0]
    prep_ref, p_ref, carry_ref = refs[:3]
    if prefixed:
        for r in range(0, before, PAD):
            p_ref[r : r + PAD, :] = before_ref[r : r + PAD, :]
    tb, fr, fc, qr, qc, rhs, inv, pa, pb, drive = refs[3:]
    index, half = lax.axis_index("layer"), lax.axis_size("layer") // 2
    upper = index >= half
    middle = (index == half - 1) | (index == half)
    length, width = prep_ref.shape[1:]

    def total(at):
        value = sums[0][:, at, :]
        for ref in sums[1:]:
            value = value + ref[:, at, :]
        return value

    if first:
        for r in range(0, length, PAD):
            tb[:, PAD + r : 2 * PAD + r, :] = total(slice(PAD + r, 2 * PAD + r))
        slab = total(slice(0, PAD))[0]
        p_ref[length - 2 * PAD : length - PAD, :] = jnp.where(middle, slab, 0.0)
    else:
        n = length - 2 * PAD
        at = jnp.where(upper, 2 * PAD, 0) + PAD
        for r in range(0, n, PAD):
            tb[:, pl.ds(pl.multiple_of(at + r, PAD), PAD), :] = total(slice(r, r + PAD))
        at = pl.multiple_of(jnp.where(upper, 0, n) + PAD, PAD)
        tb[:, pl.ds(at, 2 * PAD), :] = carry_in[...]
    tb[:, PAD + length : 2 * PAD + length, :] = jnp.zeros((2, PAD, width), f32)
    if last:
        carry_ref[...] = jnp.zeros_like(carry_ref)
    else:
        at = pl.multiple_of(jnp.where(upper, length - 2 * PAD, 0) + PAD, PAD)
        carry_ref[...] = tb[:, pl.ds(at, 2 * PAD), :]

    edge = last_lane((PAD, width))
    zero = jnp.zeros((PAD, width), f32)
    fr[0:PAD, :] = zero
    qr[0:PAD, :] = zero
    for ref in (pa, pb):
        ref[0:PAD, :] = zero
        ref[PAD + length : 2 * PAD + length, :] = zero
    drive[length : length + PAD, :] = zero
    thick = [thick_ref[z] for z in range(thick_ref.shape[0])]
    for r in range(0, length, PAD):
        top, bottom = prep_ref[0, r : r + PAD, :], prep_ref[4, r : r + PAD, :]
        height = zero
        for z, t in enumerate(thick):
            height = height + jnp.where((top <= z) & (bottom > z), t, 0.0)
        drive[r : r + PAD, :] = buoyancy_scale * height
    for r in range(0, length, PAD):
        here, down = slice(PAD + r, 2 * PAD + r), slice(PAD + r + 1, 2 * PAD + r + 1)
        t, b, d = tb[0, here, :], tb[1, here, :], drive[r : r + PAD, :]
        fr[here, :] = harmonic(t, tb[0, down, :])
        fc[r : r + PAD, :] = jnp.where(edge, 0.0, harmonic(t, next_col(t)))
        below = drive[r + 1 : r + PAD + 1, :]
        qr[here, :] = harmonic(b, tb[1, down, :]) * (below - d)
        qc[r : r + PAD, :] = jnp.where(edge, 0.0, harmonic(b, next_col(b)) * (next_col(d) - d))
        pa[here, :] = prep_ref[3, r : r + PAD, :]
    for r in range(0, length, PAD):
        here, up = slice(PAD + r, 2 * PAD + r), slice(PAD + r - 1, 2 * PAD + r - 1)
        flow = qc[r : r + PAD, :]
        face = fc[r : r + PAD, :]
        rhs[r : r + PAD, :] = (
            prep_ref[2, r : r + PAD, :] + (qr[here, :] - qr[up, :]) + (flow - prev_col(flow))
        )
        diagonal = prep_ref[1, r : r + PAD, :] + fr[up, :] + fr[here, :] + prev_col(face) + face
        inv[r : r + PAD, :] = 1.0 / diagonal
    source, target = pa, pb
    for sweep in range(SWEEPS):
        final = sweep == SWEEPS - 1
        lo, hi = (PAD, length if last else length - PAD) if final else (0, length)
        for r in range(lo, hi, PAD):
            here = slice(PAD + r, 2 * PAD + r)
            up = slice(PAD + r - 1, 2 * PAD + r - 1)
            down = slice(PAD + r + 1, 2 * PAD + r + 1)
            p, face = source[here, :], fc[r : r + PAD, :]
            value = (
                rhs[r : r + PAD, :]
                + fr[up, :] * source[up, :]
                + fr[here, :] * source[down, :]
                + prev_col(face * p)
                + face * next_col(p)
            ) * inv[r : r + PAD, :]
            if final:
                p_ref[before + r - PAD : before + r, :] = jnp.where(middle, value, 0.0)
            else:
                target[here, :] = value
        source, target = target, source


def solve(first, last, thick_all, sums, carry, prep, before, after):
    length, width = prep.shape[1:]
    prefixed = before is not None
    p_rows = length - PAD if first or last else length - 2 * PAD
    p_rows += before.shape[0] if prefixed else 0
    args = [thick_all] + list(sums) + ([] if first else [carry]) + ([before] if prefixed else []) + [prep]
    tall = pltpu.VMEM((length + 2 * PAD, width), f32)
    flat = pltpu.VMEM((length, width), f32)
    return call(
        functools.partial(solve_kernel, first, last, prefixed, len(sums)), args, [SCALARS] + [WHOLE] * (len(args) - 1), after,
        out_specs=(WHOLE, WHOLE),
        out_shape=(
            jax.ShapeDtypeStruct((p_rows, width), f32),
            jax.ShapeDtypeStruct((2, 2 * PAD, width), f32),
        ),
        scratch_shapes=[pltpu.VMEM((2, length + 2 * PAD, width), f32), tall, flat, tall, flat, flat, flat, tall, tall, tall],
        compiler_params=params(6 * scale()),
        name="solve",
    )


def local_heads(first, thick_ref, cap, plume):
    over, out = None, []
    for z in range(thick_ref.shape[0]):
        t = thick_ref[z]
        gas = (cap <= first + z) & (plume > first + z)
        mass = jnp.where(gas, t * gas_density, t * brine_density)
        mid = 0.5 * mass
        out.append(gravity_scale * (mid if over is None else over + mid))
        over = mass if over is None else over + mass
    return out


def cells_kernel(final_piece, perm_ref, mob_ref, cap_ref, plume_ref, perm_n, mob_n, cap_n, thick_ref, high_ref, hr_ref, hc_ref, g_ref, gh_ref, cond):
    layers, rows, width = perm_ref.shape
    first = lax.axis_index("layer") * layers
    for r in range(0, rows, PAD):
        rr = slice(r, r + PAD)
        cap, plume = cap_ref[rr, :], plume_ref[rr, :]
        for z in range(layers):
            cond[z, rr, :] = conduct_of(perm_ref[z, rr, :], mob_ref[z, rr, :], thick_ref[z], first + z, cap)
        for z, h in enumerate(local_heads(first, thick_ref, cap, plume)):
            g_ref[z, rr, :] = h
    cap = cap_n[...]
    for z in range(layers):
        cond[z, rows : rows + PAD, :] = conduct_of(perm_n[z], mob_n[z], thick_ref[z], first + z, cap)
    if final_piece:
        @pl.when(pl.program_id(0) == pl.num_programs(0) - 1)
        def _():
            for z in range(layers):
                cond[z, rows : rows + 1, :] = high_ref[7 + z // PAD, z % PAD : z % PAD + 1, :]
            cap, plume = high_ref[2].astype(jnp.int32), high_ref[3].astype(jnp.int32)
            for z, h in enumerate(local_heads(first, thick_ref, cap, plume)):
                gh_ref[z] = h
    else:
        gh_ref[...] = jnp.zeros_like(gh_ref)

    edge = last_lane((PAD, width))
    for z in range(layers):
        for r in range(0, rows, PAD):
            c = cond[z, r : r + PAD, :]
            hr_ref[z, r : r + PAD, :] = harmonic(c, cond[z, r + 1 : r + PAD + 1, :])
            hc_ref[z, r : r + PAD, :] = jnp.where(edge, 0.0, harmonic(c, next_col(c)))


def cells(perm, mob, cap, plume, thick, high, base, steps, rows, after):
    layers, height, width = perm.shape
    per = rows // PAD
    nxt = lambda i: jnp.minimum((base + i + 1) * per, height // PAD - 1)
    spec3 = pl.BlockSpec((layers, rows, width), lambda i: (0, base + i, 0))
    spec2 = pl.BlockSpec((rows, width), lambda i: (base + i, 0))
    next3 = pl.BlockSpec((layers, PAD, width), lambda i: (0, nxt(i), 0))
    next2 = pl.BlockSpec((PAD, width), lambda i: (nxt(i), 0))
    out3 = pl.BlockSpec((layers, rows, width), lambda i: (0, i, 0))
    full = jax.ShapeDtypeStruct((layers, rows * steps, width), f32)
    final = (base + steps) * rows == height
    return call(
        functools.partial(cells_kernel, final), (perm, mob, cap, plume, perm, mob, cap, thick, high),
        [spec3, spec3, spec2, spec2, next3, next3, next2, SCALARS, pl.BlockSpec(high.shape, lambda i: (0, 0, 0))],
        after,
        grid=(steps,),
        out_specs=(out3, out3, out3, pl.BlockSpec((layers, PAD, width), lambda i: (0, 0, 0))),
        out_shape=(full, full, full, jax.ShapeDtypeStruct((layers, PAD, width), f32)),
        scratch_shapes=[pltpu.VMEM((layers, rows + PAD, width), f32)],
        compiler_params=params(8, 1),
        name="cells",
    )


def tops_kernel(layers, thick_ref, cap_ref, plume_ref, high_ref, out_ref):
    first = lax.axis_index("layer") * layers
    thick = [jnp.where(z < first, thick_ref[z], 0.0) for z in range(thick_ref.shape[0])]

    def value(cap, plume):
        over = jnp.zeros(cap.shape, f32)
        for z, t in enumerate(thick):
            over = over + jnp.where((cap <= z) & (plume > z), gas_density * t, brine_density * t)
        return gravity_scale * over

    height = cap_ref.shape[0]

    def step(g, _):
        at = pl.ds(pl.multiple_of(g * PAD, PAD), PAD)
        out_ref[at, :] = value(cap_ref[at, :], plume_ref[at, :])
        return 0

    lax.fori_loop(0, height // PAD, step, 0)
    out_ref[height : height + PAD, :] = value(high_ref[2].astype(jnp.int32), high_ref[3].astype(jnp.int32))


def tops(layers, thick_all, cap, plume, high, after):
    height, width = cap.shape
    return call(
        functools.partial(tops_kernel, layers), (thick_all, cap, plume, high),
        [SCALARS, WHOLE, WHOLE, WHOLE], after,
        out_specs=WHOLE,
        out_shape=jax.ShapeDtypeStruct((height + PAD, width), f32),
        compiler_params=params(3),
        name="tops",
    )


def output_kernel(plan, chunks, groups, pieces, spans, fresh, *refs):
    count = plan.count
    arrived = []
    for _ in range(1 + max(c[2] for c in chunks)):
        near, far = refs[: groups[0]], refs[groups[0] : sum(groups)]
        refs = refs[sum(groups) :]
        arrived.append((near, far))
    parts = [arrived[c[2]] for c in chunks]
    cells_refs = [refs[3 * i : 3 * i + 3] for i in range(len(pieces))]
    refs = refs[3 * len(pieces) :]
    gh_ref, top_ref, refs = refs[0], refs[1], refs[2:]
    if not fresh:
        refs = refs[3:]
    outs, refs = refs[:3], refs[3:]
    pfull, cp, slots, sems = refs
    layers, block, _ = slots.shape[2:]
    upper = upper_half()

    def summed(group, r):
        value = group[0][r : r + PAD, :]
        for ref in group[1:]:
            value = value + ref[r : r + PAD, :]
        return value

    for (j, skip, _), (near, far) in zip(chunks, parts):
        near, far = [[x.at[pl.ds(skip, x.shape[0] - skip)] for x in g] for g in (near, far)]
        last = j == count - 1
        a, b, length = plan.window(j)
        n = length - (PAD if last else 2 * PAD)

        def place(low, high, a=a, b=b, n=n, last=last):
            for r in range(0, n, PAD):
                if not (last and r == n - PAD):
                    at = a + PAD + r
                    pfull[at : at + PAD, :] = summed(low, r) + top_ref[at : at + PAD, :]
                at = b + PAD + r
                pfull[at : at + PAD, :] = summed(high, r) + top_ref[at : at + PAD, :]

        @pl.when(upper)
        def _():
            place(far, near)

        @pl.when(~upper)
        def _():
            place(near, far)

    def piece_of(row):
        base = 0
        for i, size in enumerate(pieces):
            if row < base + size:
                return cells_refs[i], row - base
            base += size
        return None, None

    blocks = []
    for lo, hi in spans:
        while lo < hi:
            base = 0
            for size in pieces:
                if lo < base + size:
                    break
                base += size
            end = min(hi, base + size, lo + block)
            blocks.append((lo, end))
            lo = end

    copies = {}
    for k, (lo, hi) in enumerate(blocks):
        slot, rows = k % 2, hi - lo
        if k >= 2:
            for c in copies.pop(k - 2):
                c.wait()
        (hr, hc, g), off = piece_of(lo)
        (ng, noff) = piece_of(hi)
        for z in range(layers):
            for r in range(0, rows, PAD):
                value = pfull[lo + r : lo + r + PAD, :] + g[z, off + r : off + r + PAD, :]
                cp[z, r : r + PAD, :] = value
                slots[slot, 0, z, r : r + PAD, :] = value
            beyond = gh_ref[z] if ng is None else ng[2][z, noff : noff + PAD, :]
            cp[z, rows : rows + PAD, :] = pfull[hi : hi + PAD, :] + beyond
            for r in range(0, rows, PAD):
                here = cp[z, r : r + PAD, :]
                at = slice(off + r, off + r + PAD)
                slots[slot, 1, z, r : r + PAD, :] = hr[z, at, :] * (here - cp[z, r + 1 : r + PAD + 1, :])
                slots[slot, 2, z, r : r + PAD, :] = hc[z, at, :] * (here - next_col(here))
        copies[k] = [
            pltpu.make_async_copy(
                slots.at[slot, i, :, 0:rows, :], outs[i].at[:, lo:hi, :], sems.at[slot, i]
            )
            for i in range(3)
        ]
        for c in copies[k]:
            c.start()
    for k in sorted(copies):
        for c in copies[k]:
            c.wait()


def outputs(plan, chunks, parts, pieces, gh, top, spans, done, after):
    layers, _, width = pieces[0][0].shape
    groups = (len(parts[0][0]), len(parts[0][1]))
    args = [x for part in parts[: 1 + max(c[2] for c in chunks)] for group in part for x in group]
    args += [x for piece in pieces for x in piece]
    args += [gh, top]
    specs = [WHOLE] * len(args)
    aliases = {}
    if done is not None:
        aliases = {len(args) + i: i for i in range(3)}
        args += list(done)
        specs += [ANY] * 3
    block = 64
    full = jax.ShapeDtypeStruct((layers, plan.height, width), f32)
    sizes = [piece[0].shape[1] for piece in pieces]
    return call(
        functools.partial(output_kernel, plan, chunks, groups, sizes, spans, done is None), args, specs, after,
        out_specs=(ANY, ANY, ANY),
        out_shape=(full, full, full),
        input_output_aliases=aliases,
        scratch_shapes=[
            pltpu.VMEM((plan.height + PAD, width), f32),
            pltpu.VMEM((layers, block + PAD, width), f32),
            pltpu.VMEM((2, 3, layers, block, width), f32),
            pltpu.SemaphoreType.DMA((2, 3)),
        ],
        compiler_params=params(10 * scale()),
        name="outputs",
    )


def local(permeability, mobility, thickness, caprock, plume, storage, source, pressure_old):
    keep = lambda x: pltpu.with_memory_space_constraint(x, pltpu.HBM)
    permeability, mobility, cap, plm = [keep(x) for x in (permeability, mobility, caprock, plume)]
    layers, height, _ = permeability.shape
    count = lax.axis_size("layer")
    tiles = lax.axis_size("area")
    half = count // 2
    depth = layers * count
    plan = Plan(height)
    fields = (caprock, plume, storage, source, pressure_old)

    forward = [(i, i + 1) for i in range(tiles - 1)]
    backward = [(i + 1, i) for i in range(tiles - 1)]
    mirror = lambda pairs: pairs + [(count - 1 - a, count - 1 - b) for a, b in pairs]
    inward = [mirror([(h, h + 1)]) for h in range(half - 1)]
    near_in = [mirror([(h, half - 1)]) for h in range(half - 1)]
    far_in = [mirror([(h, half)]) for h in range(half - 1)]
    swap = mirror([(half - 1, half)])
    out_near = [mirror([(half - 1, h)]) for h in range(half - 1)]
    out_far = [mirror([(half, h)]) for h in range(half - 1)]

    def send(x, pairs, axis="layer"):
        return lax.ppermute(x, axis, pairs)


    def chain(own):
        terms = [own]
        for pairs in inward:
            total = terms[0] if len(terms) == 1 else terms[0] + terms[1]
            terms = [own, send(total, pairs)]
        return terms

    def spread(value):
        near = [value] + [send(value, pairs) for pairs in out_near]
        far = [send(value, swap)]
        far += [send(value, pairs) for pairs in out_far]
        return near, far

    sums = lambda j, halo, after: chunk_sums(
        plan, j, permeability, mobility, thickness, cap, plm, halo, after
    )
    own0 = sums(0, None, [])
    edge_first, edge_last = edges(
        permeability, mobility, thickness, [keep(x) for x in fields], [own0]
    )
    low = send(edge_last, forward, "area")
    high = send(edge_first, backward, "area")
    own1 = sums(1, None, [edge_first])
    terms0, terms1 = chain(own0), chain(own1)
    near2, far2 = sums(2, jnp.stack([low[0:2], high[0:2]]), [own1])
    final = [near2]
    final += [send(near2, pairs) for pairs in near_in]
    final += [send(far2, pairs) for pairs in far_in]
    final += [send(far2, swap)]

    block = 64
    steps = height // block
    cuts = [steps * 3 // 8, steps * 6 // 8, steps]
    cell = lambda i, after: cells(
        permeability, mobility, cap, plm, thickness, high,
        cuts[i - 1] if i else 0, cuts[i] - (cuts[i - 1] if i else 0), block, after,
    )

    pieces = [cell(0, [near2])]
    near0, far0 = merge(plan, terms0, [pieces[0][3]])
    sums0 = [near0, send(far0, swap)]
    preps = prepare(plan, fields, low, high, [far0])
    pieces.append(cell(1, [preps[0]]))
    near1, far1 = merge(plan, terms1, [pieces[1][3]])
    sums1 = [near1, send(far1, swap)]
    pieces.append(cell(2, [far1]))

    thick_all = sum(x[0, 0, 0:depth] for x in sums0)
    value0, carry = solve(True, False, thick_all, sums0, None, preps[0], None, [pieces[2][3]])
    value1, carry = solve(False, False, thick_all, sums1, carry, preps[1], value0, [])
    part0 = spread(value1)
    value2, _ = solve(False, True, thick_all, final, carry, preps[2], None, [value1])
    parts = [part0, spread(value2)]
    slab = plan.sizes[0] - PAD
    thick_top = sum(x[slab, 0:depth] for x in part0[0])
    top = tops(layers, thick_top, caprock, plume, high, [value2])

    cell_fields = [p[:3] for p in pieces]
    gh = pieces[2][3]
    reach = plan.inner[2]
    lo, hi = plan.half - reach + PAD, plan.half + reach - 2 * PAD
    chunks = [(0, 0, 0), (1, value0.shape[0], 0), (2, 0, 1)]
    done = outputs(plan, chunks[:2], parts, cell_fields, gh, top, [(lo, hi)], None, [value2])
    return outputs(plan, chunks, parts, cell_fields, gh, top, [(0, lo), (hi, height)], done, [])


def solution(mesh):
    in_specs = (
        P("layer", "area", None),
        P("layer", "area", None),
        P("layer"),
        P("area", None),
        P("area", None),
        P("area", None),
        P("area", None),
        P("area", None),
    )
    out_specs = (P("layer", "area", None), P("layer", "area", None), P("layer", "area", None))

    return jax.shard_map(local, mesh=mesh, in_specs=in_specs, out_specs=out_specs, check_vma=False)
```
